32 devices in a mesh: dp: 16 (over z, x, core), tensor: 2 (over y).
Axes of the slice: x: 2, y: 2, z: 4, core: 2. Of those that a mesh axis runs over, the one named last changes fastest.
Arguments:
- tokens: bfloat16 [4096, 2048], P(('dp', 'tensor')), may hold values from -12 to 12
- positions: int32 [4096], P('dp'), may hold values from 0 to 255, as said below
- attn_gain: bfloat16 [2048], P('dp'), may hold values from 0.25 to 1.75
- q_weight: bfloat16 [2048, 2048], P('dp', 'tensor'), may hold values from -0.125 to 0.125
- k_weight: bfloat16 [2048, 1024], P('dp', 'tensor'), may hold values from -0.125 to 0.125
- v_weight: bfloat16 [2048, 1024], P('dp', 'tensor'), may hold values from -0.125 to 0.125
- q_gain: bfloat16 [128], P('dp'), may hold values from 0.25 to 1.75
- k_gain: bfloat16 [128], P('dp'), may hold values from 0.25 to 1.75
- o_weight: bfloat16 [2048, 2048], P('tensor', 'dp'), may hold values from -0.5 to 0.5
- mlp_gain: bfloat16 [2048], P('dp'), may hold values from 0.25 to 1.75
- gate_weight: bfloat16 [2048, 6144], P('dp', 'tensor'), may hold values from -0.125 to 0.125
- up_weight: bfloat16 [2048, 6144], P('dp', 'tensor'), may hold values from -0.125 to 0.125
- down_weight: bfloat16 [6144, 2048], P('tensor', 'dp'), may hold values from -0.078125 to 0.078125
- cotangent: bfloat16 [4096, 2048], P(('dp', 'tensor')), may hold values from -6 to 6
Outputs:
- output: bfloat16 [4096, 2048], P(('dp', 'tensor'))
- tokens_grad: float32 [4096, 2048], P(('dp', 'tensor'))
- attn_gain_grad: float32 [2048], P('dp')
- q_weight_grad: float32 [2048, 2048], P('dp', 'tensor')
- k_weight_grad: float32 [2048, 1024], P('dp', 'tensor')
- v_weight_grad: float32 [2048, 1024], P('dp', 'tensor')
- q_gain_grad: float32 [128], P('dp')
- k_gain_grad: float32 [128], P('dp')
- o_weight_grad: float32 [2048, 2048], P('tensor', 'dp')
- mlp_gain_grad: float32 [2048], P('dp')
- gate_weight_grad: float32 [2048, 6144], P('dp', 'tensor')
- up_weight_grad: float32 [2048, 6144], P('dp', 'tensor')
- down_weight_grad: float32 [6144, 2048], P('tensor', 'dp')
The draws below stay inside these ranges and needn't reach their ends.
Inputs may be any that keep to these rules, and one draw needn't show every extreme that they name: Within each sequence of 256 tokens, positions count up by one from 0 and restart at 0 at up to three places.
All inputs are finite; a program needn't handle non-finite values.
Results may differ from the reference program's by a relative error of at most 0.017.
Values may be sent and summed in bfloat16 or wider, within the bound.
No kernel may reach another device: no remote copies, remote signals or barrier semaphores. Data moves between devices by JAX's collectives and lax.ppermute only.
A program may use at most 256 MiB of HBM per device.

```python
import math
import jax
import jax.numpy as jnp
from jax import lax

D = 2048
HEADS = 16
KV_HEADS = 8
HEAD = 128
FF = 6144
LEN = 256
TOKENS = 4096


def draw_tokens(key, part):
    row_scale = jnp.exp(jax.random.uniform(jax.random.fold_in(key, 31), (TOKENS, 1), jnp.float32, math.log(0.3), math.log(3.0)))
    entries = jax.random.normal(jax.random.fold_in(key, 34), (TOKENS, D), jnp.float32)
    return jnp.clip(entries * row_scale, -12.0, 12.0).astype(jnp.bfloat16)


def draw_positions(key, part):
    seq_count = TOKENS // LEN
    cut_points = jax.random.randint(jax.random.fold_in(key, 41), (seq_count, 3), 1, LEN)
    first_row = jnp.arange(seq_count)[:, None] == 0
    cut_points = jnp.where(first_row, LEN, cut_points)
    position_index = jnp.arange(LEN)[None, :, None]
    doc_starts = jnp.max(jnp.where(cut_points[:, None, :] <= position_index, cut_points[:, None, :], 0), axis=2)
    return (jnp.arange(LEN)[None, :] - doc_starts).reshape(seq_count * LEN).astype(jnp.int32)


def strengthened(values, rng, source, target, shards_of, factor):
    owner, partner = [(jnp.arange(values.shape[position]) // (values.shape[position] // shards_of)).reshape([-1 if axis == position else 1 for axis in range(values.ndim)]) for position in (source, target)]
    chosen = jax.random.permutation(rng, shards_of)[partner]
    strong = (owner == chosen) | (owner == (partner + shards_of // 2) % shards_of)
    return jnp.where(strong, factor * values, values)


def block_levels(rng, extent, pieces, low, top_value):
    level, own = 1.0, jax.random.fold_in(rng, 6)
    for dim, shards_of in pieces:
        heights = jnp.exp(jax.random.uniform(jax.random.fold_in(own, dim), (shards_of,), jnp.float32, low / len(pieces), top_value / len(pieces)))
        level = level * jnp.repeat(heights, extent[dim] // shards_of).reshape([-1 if axis == dim else 1 for axis in range(len(extent))])
    return level


def gaussian(stream_key, extent, width, reach, shards=(), held_as=jnp.bfloat16):
    values = jax.random.normal(stream_key, extent, jnp.float32) * width
    if len(shards) > 0:
        values = block_levels(stream_key, extent, shards, -0.22, 0.18) * values
    return jnp.clip(values, min=-reach, max=reach).astype(held_as)


def bell_draw_with(own_key, dims, spread, most, cuts, heavy, kind=jnp.bfloat16):
    array = spread * jax.random.normal(own_key, dims, jnp.float32)
    if cuts:
        array = array * block_levels(own_key, dims, cuts, -0.22, 0.18)
    return jnp.clip(strengthened(array, jax.random.fold_in(own_key, 3), *heavy), -most, most).astype(kind)


def setup_inputs(seed: int = 0) -> dict:
    arg_keys = jax.random.split(jax.random.key(seed), 15)
    return {
        "tokens": draw_tokens(jax.random.fold_in(arg_keys[14], 71), 0),
        "positions": draw_positions(jax.random.fold_in(arg_keys[14], 71), 0),
        "attn_gain": jnp.clip(1.0 + 0.15 * jax.random.normal(arg_keys[2], (D,), jnp.float32), 0.25, 1.75).astype(jnp.bfloat16),
        "q_weight": gaussian(arg_keys[3], (D, HEADS * HEAD), D ** -0.5, 0.125, ((0, 16), (1, 2))),
        "k_weight": gaussian(arg_keys[4], (D, KV_HEADS * HEAD), D ** -0.5, 0.125, ((0, 16), (1, 2))),
        "v_weight": gaussian(arg_keys[5], (D, KV_HEADS * HEAD), D ** -0.5, 0.125, ((0, 16), (1, 2))),
        "q_gain": jnp.clip(1.0 + 0.15 * jax.random.normal(arg_keys[6], (HEAD,), jnp.float32), 0.25, 1.75).astype(jnp.bfloat16),
        "k_gain": jnp.clip(1.0 + 0.15 * jax.random.normal(arg_keys[7], (HEAD,), jnp.float32), 0.25, 1.75).astype(jnp.bfloat16),
        "o_weight": gaussian(arg_keys[8], (HEADS * HEAD, D), HEAD ** -0.5, 0.5, ((0, 2), (1, 16))),
        "mlp_gain": jnp.clip(1.0 + 0.15 * jax.random.normal(arg_keys[9], (D,), jnp.float32), 0.25, 1.75).astype(jnp.bfloat16),
        "gate_weight": gaussian(arg_keys[10], (D, FF), D ** -0.5, 0.125, ((0, 16), (1, 2))),
        "up_weight": gaussian(arg_keys[11], (D, FF), D ** -0.5, 0.125, ((0, 16), (1, 2))),
        "down_weight": gaussian(arg_keys[12], (FF, D), FF ** -0.5, 0.078125, ((0, 2), (1, 16))),
        "cotangent": bell_draw_with(arg_keys[13], (TOKENS, D), 1.0, 6.0, ((0, 32),), (0, 1, 32, 2.75)),
    }


EPSILON = 1e-06
ROPE_THETA = 1000000.0

@jax.custom_vjp
def low(v):
    return lax.optimization_barrier(v.astype(jnp.bfloat16)).astype(jnp.float32)

@jax.custom_vjp
def low_back(v):
    return v

def low_keep(v):
    return (low(v), None)

def low_pass(kept, grad):
    return (grad,)

def back_keep(v):
    return (v, None)

def back_low(kept, grad):
    return (low(grad),)
low.defvjp(low_keep, low_pass)
low_back.defvjp(back_keep, back_low)

def precise_dot(left, right):
    return jnp.dot(left, right, precision=lax.Precision.HIGHEST, preferred_element_type=jnp.float32)

def rms_norm(values, gain):
    return values * lax.rsqrt(lax.optimization_barrier(jnp.mean(values * values, axis=-1, keepdims=True)) + EPSILON) * gain

def rotation(positions):
    half_size = HEAD // 2
    frequency = ROPE_THETA ** (-jnp.arange(half_size, dtype=jnp.float32) * 2.0 / HEAD)
    angles = positions.astype(jnp.float32)[:, None] * frequency[None, :]
    return (jnp.cos(angles)[:, None, :], jnp.sin(angles)[:, None, :])

def rotate(values, cosine_table, sine_table):
    half_size = values.shape[-1] // 2
    first_half = values[..., :half_size]
    second_half = values[..., half_size:]
    return jnp.concatenate([first_half * cosine_table - second_half * sine_table, second_half * cosine_table + first_half * sine_table], axis=-1)

def sequence_layer(params, inputs, positions):
    attn_gain, q_weight, k_weight, v_weight, q_gain, k_gain, o_weight, mlp_gain, gate_weight, up_weight, down_weight = params
    seq_length = inputs.shape[0]
    group_size = HEADS // KV_HEADS
    normed = low(rms_norm(inputs, attn_gain))
    queries = low_back(precise_dot(normed, q_weight)).reshape(seq_length, HEADS, HEAD)
    keys_pre = low_back(precise_dot(normed, k_weight)).reshape(seq_length, KV_HEADS, HEAD)
    values = low(low_back(precise_dot(normed, v_weight))).reshape(seq_length, KV_HEADS, HEAD)
    cosine_table, sine_table = rotation(positions)
    q_rot = low(rotate(rms_norm(queries, q_gain), cosine_table, sine_table))
    k_rot = low(rotate(rms_norm(keys_pre, k_gain), cosine_table, sine_table))
    k_wide = jnp.repeat(k_rot, group_size, axis=1)
    v_wide = jnp.repeat(values, group_size, axis=1)
    raw_scores = jnp.einsum('qhd,khd->hqk', q_rot, k_wide, precision=lax.Precision.HIGHEST)
    scores = low_back(raw_scores * HEAD ** (-0.5))
    causal = jnp.arange(seq_length)[:, None] >= jnp.arange(seq_length)[None, :]
    scores = jnp.where(causal[None], scores, -jnp.inf)
    row_max = lax.optimization_barrier(jnp.max(scores, axis=-1, keepdims=True))
    exponent = jnp.exp(scores - row_max)
    attn_probs = low(exponent / lax.optimization_barrier(jnp.sum(exponent, axis=-1, keepdims=True)))
    attended = jnp.einsum('hqk,khd->qhd', attn_probs, v_wide, precision=lax.Precision.HIGHEST)
    attended = low(low_back(attended.reshape(seq_length, HEADS * HEAD)))
    mid = inputs + low_back(precise_dot(attended, o_weight))
    mid_normed = low(rms_norm(mid, mlp_gain))
    gate_pre = low_back(precise_dot(mid_normed, gate_weight))
    up_pre = low_back(precise_dot(mid_normed, up_weight))
    hidden = low(gate_pre * jax.nn.sigmoid(gate_pre) * up_pre)
    return mid + precise_dot(hidden, down_weight)

def reference(tokens, positions, attn_gain, q_weight, k_weight, v_weight, q_gain, k_gain, o_weight, mlp_gain, gate_weight, up_weight, down_weight, cotangent):
    params = tuple((operand.astype(jnp.float32) for operand in (attn_gain, q_weight, k_weight, v_weight, q_gain, k_gain, o_weight, mlp_gain, gate_weight, up_weight, down_weight)))
    seq_count = TOKENS // LEN
    sequences = tokens.astype(jnp.float32).reshape(seq_count, LEN, D)
    seq_positions = positions.reshape(seq_count, LEN)

    def forward(weights, inputs):

        def single(paired):
            return sequence_layer(weights, paired[0], paired[1])
        return lax.map(jax.checkpoint(single), (inputs, seq_positions))
    outputs, pullback = jax.vjp(forward, params, sequences)
    weight_grads, input_grads = pullback(cotangent.astype(jnp.float32).reshape(seq_count, LEN, D))
    return (outputs.reshape(TOKENS, D).astype(jnp.bfloat16), input_grads.reshape(TOKENS, D), weight_grads[0], weight_grads[1], weight_grads[2], weight_grads[3], weight_grads[4], weight_grads[5], weight_grads[6], weight_grads[7], weight_grads[8], weight_grads[9], weight_grads[10])
```

```python
import functools

import jax
import jax.numpy as jnp
from jax import lax
from jax.sharding import PartitionSpec as P

HEAD = 128
EPSILON = 1e-06
ROPE_THETA = 1000000.0
RING = 4


BF = jnp.bfloat16
F32 = jnp.float32


def dot(left, right):
    return lax.dot_general(left, right, (((1,), (0,)), ((), ())), preferred_element_type=F32)


def dot_rows(left, right):
    return lax.dot_general(left, right, (((0,), (0,)), ((), ())), preferred_element_type=F32)


def dot_cols(left, right):
    return lax.dot_general(left, right, (((1,), (1,)), ((), ())), preferred_element_type=F32)


def norm_rows(values):
    scale = lax.rsqrt(jnp.mean(values * values, axis=-1, keepdims=True) + EPSILON)
    return values * scale, scale


def norm_back(grad_in, values_hat, scale, gain):
    weighted = grad_in * gain
    return scale * (weighted - values_hat * jnp.mean(weighted * values_hat, axis=-1, keepdims=True))


def rotate(values, cosine, sine):
    half = values.shape[-1] // 2
    a, b = values[..., :half], values[..., half:]
    return jnp.concatenate([a * cosine - b * sine, b * cosine + a * sine], axis=-1)


def after(value, *others):
    return lax.optimization_barrier((value, *others))[0]


class Place:
    def __init__(self, count):
        self.count = count
        self.sizes = {"z": RING, "x": count // (2 * RING), "c": 2}
        self.m = self.sizes["x"]
        index = lax.axis_index("dp")
        self.z = index // (2 * self.m)
        self.x = (index // 2) % self.m
        self.c = index % 2
        self.y = lax.axis_index("tensor")

    def split(self, i):
        return {"z": i // (2 * self.m), "x": (i // 2) % self.m, "c": i % 2}

    def join(self, d):
        return (d["z"] * self.m + d["x"]) * 2 + d["c"]

    def ahead(self, value, digit, step=1):
        pairs = []
        for i in range(self.count):
            d = self.split(i)
            d[digit] = (d[digit] - step) % self.sizes[digit]
            pairs.append((i, self.join(d)))
        return lax.ppermute(value, "dp", pairs)

    def other(self, value):
        return lax.ppermute(value, "tensor", [(0, 1), (1, 0)])

    def roll(self, array, digit_value, size, width, sign):
        if size == 1:
            return array
        group = size * width
        cases = []
        for value in range(size):
            cut = (value if sign > 0 else (size - value) % size) * width
            parts = []
            for start in range(0, array.shape[1], group):
                parts += [array[:, start + cut : start + group], array[:, start : start + cut]]
            parts = [p for p in parts if p.shape[1]]
            cases.append(jnp.concatenate(parts, axis=1) if len(parts) > 1 else parts[0])
        if size == 2:
            return jnp.where(digit_value == 0, cases[0], cases[1])
        return lax.select_n(digit_value, *cases)

    def swap(self, array, first, second, width):
        if first == 1 or second == 1:
            return array
        parts = []
        for start in range(0, array.shape[1], first * second * width):
            for j in range(second):
                for i in range(first):
                    at = start + (i * second + j) * width
                    parts.append(array[:, at : at + width])
        return jnp.concatenate(parts, axis=1)

    def plain_to_shared(self, a):
        w = a.shape[1] // self.count
        a = self.swap(a, self.m, 2, w)
        a = self.roll(a, self.x, self.m, w, 1)
        return self.roll(a, self.c, 2, self.m * w, 1)

    def shared_to_plain(self, a):
        w = a.shape[1] // self.count
        a = self.roll(a, self.c, 2, self.m * w, -1)
        a = self.roll(a, self.x, self.m, w, -1)
        return self.swap(a, 2, self.m, w)

    def shared_to_own(self, a):
        return self.roll(a, self.z, RING, a.shape[1] // RING, 1)

    def own_to_shared(self, a):
        return self.roll(a, self.z, RING, a.shape[1] // RING, -1)

    def spread_xc(self, block):
        parts = [block]
        for _ in range(self.m - 1):
            parts.append(self.ahead(parts[-1], "x"))
        mine = jnp.concatenate(parts, axis=0)
        return jnp.concatenate([mine, self.ahead(mine, "c")], axis=0)

    def sum_xc(self, block, sent=BF):
        half = block.shape[0] // 2
        block = block[:half].astype(F32) + self.ahead(block[half:].astype(sent), "c").astype(F32)
        rows = half // self.m
        total = None
        for k in [*range(1, self.m), 0]:
            own = block[k * rows : (k + 1) * rows]
            total = own if total is None else own + self.ahead(total.astype(sent), "x").astype(F32)
        return total

    def ring_sum(self, pieces, sent=BF):
        total = pieces[1]
        for k in (2, 3, 0):
            total = pieces[k].astype(F32) + self.ahead(total.astype(sent), "z").astype(F32)
        return total


def attention_forward(place, qkv, q_gain, k_gain, cosine, sine, causal, q_cols, kv_cols):
    length = qkv.shape[0]
    heads, kv_heads = q_cols // HEAD, kv_cols // HEAD
    queries = qkv[:, :q_cols].reshape(length, heads, HEAD)
    keys = qkv[:, q_cols : q_cols + kv_cols].reshape(length, kv_heads, HEAD)
    values = qkv[:, q_cols + kv_cols :].astype(BF).reshape(length, kv_heads, HEAD)
    q_hat, q_scale = norm_rows(queries)
    k_hat, k_scale = norm_rows(keys)
    q_rot = rotate(q_hat * q_gain, cosine, sine).astype(BF)
    k_rot = rotate(k_hat * k_gain, cosine, sine).astype(BF)
    group = heads // kv_heads
    q_heads = q_rot.reshape(length, kv_heads, group, HEAD).transpose(1, 2, 0, 3)
    k_heads = k_rot.transpose(1, 0, 2)
    v_heads = values.transpose(1, 0, 2)
    scores = jnp.einsum("hgqd,hsd->hgqs", q_heads, k_heads, preferred_element_type=F32) * HEAD**-0.5
    scores = jnp.where(causal[None, None], scores, -jnp.inf)
    exponent = jnp.exp(scores - jnp.max(scores, axis=-1, keepdims=True))
    probs = exponent / jnp.sum(exponent, axis=-1, keepdims=True)
    attended = jnp.einsum("hgqs,hsd->hgqd", probs.astype(BF), v_heads, preferred_element_type=F32)
    attended = attended.astype(BF).transpose(2, 0, 1, 3).reshape(length, q_cols)
    return attended, (q_hat, q_scale, k_hat, k_scale, q_heads, k_heads, v_heads, probs)


def attention_backward(saved, d_attended, q_gain, k_gain, cosine, sine):
    q_hat, q_scale, k_hat, k_scale, q_heads, k_heads, v_heads, probs = saved
    length = q_hat.shape[0]
    kv_heads, group = q_heads.shape[:2]
    grad = d_attended.reshape(length, kv_heads, group, HEAD).transpose(1, 2, 0, 3)
    d_probs = jnp.einsum("hgqd,hsd->hgqs", grad, v_heads, preferred_element_type=F32)
    delta = jnp.sum(probs * d_probs, axis=-1, keepdims=True)
    d_scores = (probs * (d_probs - delta)).astype(BF)
    d_values = jnp.einsum("hgqs,hgqd->hsd", probs.astype(BF), grad, preferred_element_type=F32)
    d_qrot = jnp.einsum("hgqs,hsd->hgqd", d_scores, k_heads, preferred_element_type=F32)
    d_krot = jnp.einsum("hgqs,hgqd->hsd", d_scores, q_heads, preferred_element_type=F32)
    d_qrot = d_qrot.transpose(2, 0, 1, 3).reshape(length, kv_heads * group, HEAD) * HEAD**-0.5
    d_krot = d_krot.transpose(1, 0, 2) * HEAD**-0.5
    d_qn = rotate(d_qrot, cosine, -sine)
    d_kn = rotate(d_krot, cosine, -sine)
    q_term = jnp.sum(d_qn * q_hat, axis=(0, 1))
    k_term = jnp.sum(d_kn * k_hat, axis=(0, 1))
    d_queries = norm_back(d_qn, q_hat, q_scale, q_gain).astype(BF).reshape(length, -1)
    d_keys = norm_back(d_kn, k_hat, k_scale, k_gain).astype(BF).reshape(length, -1)
    d_values = d_values.transpose(1, 0, 2).astype(BF).reshape(length, -1)
    return jnp.concatenate([d_queries, d_keys, d_values], axis=1), q_term, k_term


def per_device(
    count,
    tokens,
    positions,
    attn_gain,
    q_weight,
    k_weight,
    v_weight,
    q_gain,
    k_gain,
    o_weight,
    mlp_gain,
    gate_weight,
    up_weight,
    down_weight,
    cotangent,
):
    place = Place(count)
    m = place.m
    part, width = tokens.shape
    rows = q_weight.shape[0]
    q_cols, kv_cols = q_weight.shape[1], k_weight.shape[1]
    units = gate_weight.shape[1] // RING
    gain_rows = q_gain.shape[0]

    packed = jnp.concatenate([attn_gain, mlp_gain, q_gain, k_gain])[None]
    packed = [packed]
    for _ in range(RING - 1):
        packed.append(place.ahead(packed[-1], "z"))
    packed = jnp.concatenate([place.spread_xc(b) for b in packed], axis=0)
    attn_own = packed[:, :rows].reshape(1, width).astype(F32)
    mlp_own = packed[:, rows : 2 * rows].reshape(1, width).astype(F32)
    slots = jnp.arange(count)
    kz, kc, kx = slots // (2 * m), (slots // m) % 2, slots % m
    held = (((place.z + kz) % RING) * m + (place.x + kx) % m) * 2 + (place.c + kc) % 2
    is_at = (held[None, :] == jnp.arange(count)[:, None]).astype(F32)
    small = packed[:, 2 * rows :].astype(F32)
    small = jnp.sum(is_at[:, :, None] * small[None], axis=1)
    q_gain_f = small[:, :gain_rows].reshape(-1)
    k_gain_f = small[:, gain_rows:].reshape(-1)

    qkv_block = jnp.concatenate([q_weight, k_weight, v_weight], axis=1)
    o_block = o_weight.T
    qkv_ring, o_ring = [qkv_block], [o_block]
    for _ in range(RING - 1):
        qkv_ring.append(place.ahead(qkv_ring[-1], "z"))
    o_ring[0] = after(o_block, qkv_ring[-1])
    for _ in range(RING - 1):
        o_ring.append(place.ahead(o_ring[-1], "z"))
    qkv_full = jnp.concatenate([place.spread_xc(b) for b in qkv_ring], axis=0)
    o_full = jnp.concatenate([place.spread_xc(b) for b in o_ring], axis=0)

    mlp_block = jnp.concatenate(
        [
            place.roll(w, place.z, RING, units, 1).reshape(rows, RING, units)
            for w in (gate_weight, up_weight, down_weight.T)
        ],
        axis=2,
    )
    mlp_block = after(mlp_block, o_ring[-1])
    mlp_full = jnp.zeros((RING, 2 * m * rows, 3 * units), BF)
    for k in range(RING):
        block = mlp_block[:, k]
        if k:
            block = place.ahead(block, "z", -k)
        mlp_full = lax.dynamic_update_slice(
            mlp_full, place.spread_xc(block)[None], ((place.z - k) % RING, 0, 0)
        )
    mlp_full = mlp_full.reshape(width, 3 * units)
    gate_up, down = mlp_full[:, : 2 * units], mlp_full[:, 2 * units :]

    tokens_own = place.shared_to_own(place.plain_to_shared(tokens))
    inputs = tokens_own.astype(F32)
    inputs_hat, inputs_scale = norm_rows(inputs)
    normed = (inputs_hat * attn_own).astype(BF)
    normed_all = jnp.concatenate([normed, place.other(normed)], axis=0)
    qkv = dot(normed_all, qkv_full)
    token_ids = jnp.concatenate([place.y * part + jnp.arange(part), (1 - place.y) * part + jnp.arange(part)])
    position_all = jnp.where(
        place.y == 0, positions, jnp.concatenate([positions[part:], positions[:part]])
    )
    half = HEAD // 2
    frequency = ROPE_THETA ** (-jnp.arange(half, dtype=F32) * 2.0 / HEAD)
    angles = position_all.astype(F32)[:, None] * frequency[None, :]
    cosine, sine = jnp.cos(angles)[:, None, :], jnp.sin(angles)[:, None, :]
    causal = token_ids[:, None] >= token_ids[None, :]
    attended, saved = attention_forward(
        place, qkv, q_gain_f, k_gain_f, cosine, sine, causal, q_cols, kv_cols
    )
    branch = dot_cols(attended, o_full)
    mid = inputs + branch[:part] + place.other(branch[part:].astype(BF)).astype(F32)
    mid_hat, mid_scale = norm_rows(mid)
    mid_normed = (mid_hat * mlp_own).astype(BF)

    def gather_tokens(block):
        ring = [block]
        for _ in range(RING - 1):
            ring.append(place.ahead(ring[-1], "z"))
        return jnp.concatenate([b for r in ring for b in (r, place.other(r))], axis=0)

    def sum_tokens(partial):
        pieces = []
        for k in range(RING):
            own = partial[2 * k * part : (2 * k + 1) * part]
            sent = partial[(2 * k + 1) * part : (2 * k + 2) * part]
            pieces.append(own.astype(F32) + place.other(sent.astype(BF)).astype(F32))
        return place.ring_sum(pieces)

    cot_shared = place.plain_to_shared(cotangent)
    cot_all = gather_tokens(after(cot_shared, mlp_block))
    mid_all = gather_tokens(place.own_to_shared(mid_normed))
    pre = dot(mid_all, gate_up)
    gate_pre, up_pre = pre[:, :units], pre[:, units:]
    sig = jax.nn.sigmoid(gate_pre)
    silu = gate_pre * sig
    hidden = (silu * up_pre).astype(BF)
    d_hidden = dot(cot_all, down)
    d_gate = (d_hidden * up_pre * sig * (1.0 + gate_pre * (1.0 - sig))).astype(BF)
    d_up = (d_hidden * silu).astype(BF)
    d_gate_up = jnp.concatenate([d_gate, d_up], axis=1)
    d_mid_normed = sum_tokens(dot_cols(d_gate_up, gate_up).astype(BF))
    out_sum = sum_tokens(after(dot_cols(hidden, down).astype(BF), d_mid_normed))
    output = place.shared_to_plain((place.own_to_shared(mid) + out_sum).astype(BF))

    d_mid_normed = place.shared_to_own(d_mid_normed)
    mlp_term = jnp.sum(d_mid_normed * mid_hat, axis=0)
    cot_own = place.shared_to_own(cot_shared)
    d_mid = cot_own.astype(F32) + norm_back(d_mid_normed, mid_hat, mid_scale, mlp_own)
    d_branch = d_mid.astype(BF)
    d_branch_all = jnp.concatenate([d_branch, place.other(d_branch)], axis=0)

    d_attended = dot(d_branch_all, o_full).astype(BF)
    d_qkv, q_term, k_term = attention_backward(saved, d_attended, q_gain_f, k_gain_f, cosine, sine)
    d_normed = dot_cols(d_qkv, qkv_full)
    d_normed = d_normed[:part] + place.other(d_normed[part:].astype(BF)).astype(F32)
    attn_term = jnp.sum(d_normed * inputs_hat, axis=0)
    tokens_grad = d_mid + norm_back(d_normed, inputs_hat, inputs_scale, attn_own)
    tokens_grad = place.shared_to_plain(place.own_to_shared(tokens_grad))

    def sum_rows(grad):
        span = 2 * m * rows
        return place.ring_sum([place.sum_xc(grad[k * span : (k + 1) * span]) for k in range(RING)])

    o_sum = sum_rows(dot_rows(d_branch_all, attended).astype(BF))
    qkv_sum = sum_rows(dot_rows(normed_all, d_qkv).astype(BF))

    mlp_grad = jnp.concatenate(
        [dot_rows(mid_all, d_gate_up).astype(BF), dot_rows(cot_all, hidden).astype(BF)], axis=1
    ).reshape(RING, 2 * m * rows, 3 * units)
    mlp_parts = []
    for k in range(RING):
        block = lax.dynamic_index_in_dim(mlp_grad, (place.z + k) % RING, 0, keepdims=False)
        block = place.sum_xc(block)
        if k:
            block = place.ahead(block.astype(BF), "z", -k).astype(F32)
        mlp_parts.append(block)
    sums = []
    for i in range(3):
        blocks = [b[:, i * units : (i + 1) * units] for b in mlp_parts]
        blocks = jnp.concatenate([blocks[0], *blocks[:0:-1]], axis=1)
        sums.append(place.roll(blocks, place.z, RING, units, -1))
    gate_sum, up_sum, down_sum = sums

    terms = jnp.concatenate(
        [
            attn_term.reshape(count, rows),
            mlp_term.reshape(count, rows),
            jnp.broadcast_to(q_term, (count, HEAD)),
            jnp.broadcast_to(k_term, (count, HEAD)),
        ],
        axis=1,
    )
    terms = terms + place.other(terms)
    span = 2 * m
    total = place.ring_sum(
        [place.sum_xc(terms[k * span : (k + 1) * span], F32) for k in range(RING)], F32
    )[0]
    attn_sum, mlp_sum = total[:rows], total[rows : 2 * rows]
    first = 2 * rows + lax.axis_index("dp") * gain_rows
    q_sum = lax.dynamic_slice(total, (first,), (gain_rows,))
    k_sum = lax.dynamic_slice(total, (first + HEAD,), (gain_rows,))

    return (
        output,
        tokens_grad,
        attn_sum,
        qkv_sum[:, :q_cols],
        qkv_sum[:, q_cols : q_cols + kv_cols],
        qkv_sum[:, q_cols + kv_cols :],
        q_sum,
        k_sum,
        o_sum.T,
        mlp_sum,
        gate_sum,
        up_sum,
        down_sum.T,
    )


def solution(mesh):
    in_specs = (
        P(("dp", "tensor"), None),
        P("dp"),
        P("dp"),
        P("dp", "tensor"),
        P("dp", "tensor"),
        P("dp", "tensor"),
        P("dp"),
        P("dp"),
        P("tensor", "dp"),
        P("dp"),
        P("dp", "tensor"),
        P("dp", "tensor"),
        P("tensor", "dp"),
        P(("dp", "tensor"), None),
    )
    out_specs = (
        P(("dp", "tensor"), None),
        P(("dp", "tensor"), None),
        P("dp"),
        P("dp", "tensor"),
        P("dp", "tensor"),
        P("dp", "tensor"),
        P("dp"),
        P("dp"),
        P("tensor", "dp"),
        P("dp"),
        P("dp", "tensor"),
        P("dp", "tensor"),
        P("tensor", "dp"),
    )
    return jax.shard_map(
        functools.partial(per_device, mesh.shape["dp"]),
        mesh=mesh,
        in_specs=in_specs,
        out_specs=out_specs,
        check_vma=False,
    )
```
